32 devices in a mesh: inp: 8 (over z, core), tm: 4 (over y, x).
Axes of the slice: x: 2, y: 2, z: 4, core: 2. Of those that a mesh axis runs over, the one named last changes fastest.
Arguments:
- samples: bfloat16 [256, 786432], P('inp', 'tm'), may hold values from -6 to 6
- tap_weights: float32 [4, 512], replicated, may hold values from -3 to 3
Outputs:
- visibilities: float32 [256, 2, 256, 256], P('tm', None, 'inp')
The draws below stay inside these ranges and needn't reach their ends.
All inputs are finite; a program needn't handle non-finite values.
Results may differ from the reference program's by a relative error of at most 0.00081.
Values may be sent and summed in bfloat16 or wider, within the bound.
A program may use at most 128 MiB of HBM per device.

```python
import math
import jax
import jax.numpy as jnp
from jax import lax

INPUTS = 256
FRAME = 512
TAPS = 4
S_DEV = 384
CHANNELS = 256
NSPEC = 1536
SAMPLES = 786432
N_TM = 4


def block_levels(stream_key, shape, cuts, smallest, largest):
    gain = 1.0
    for axis_at, shards_of in cuts:
        steps = jax.random.uniform(jax.random.fold_in(jax.random.fold_in(stream_key, 6), axis_at), (shards_of,), jnp.float32, smallest / len(cuts), largest / len(cuts))
        gain = gain * jnp.repeat(jnp.exp(steps), shape[axis_at] // shards_of).reshape((-1,) + (1,) * (len(shape) - 1 - axis_at))
    return gain


def noise(key, dims, deviation, most, pieces=(), kind=jnp.bfloat16):
    array = jax.random.normal(key, dims, jnp.float32) * deviation
    if len(pieces) > 0:
        array = block_levels(key, dims, pieces, -0.22, 0.18) * array
    return jnp.clip(array, min=-most, max=most).astype(kind)


def setup_inputs(seed: int = 0) -> dict:
    splits = jax.random.split(jax.random.key(seed), 3)
    samples = noise(splits[0], (INPUTS, SAMPLES), 1.0, 6.0, ((0, 8), (1, 4)))
    tap_weights = noise(splits[1], (TAPS, FRAME), 0.5, 3.0, (), jnp.float32)
    return dict(samples=samples, tap_weights=tap_weights)


def reference(samples, tap_weights):
    frames = samples.reshape(INPUTS, NSPEC, FRAME)
    index_n = jnp.arange(FRAME, dtype=jnp.int32)
    index_c = jnp.arange(CHANNELS, dtype=jnp.int32)
    phase = index_n[:, None] * index_c[None, :] % FRAME
    angle = phase.astype(jnp.float32) * (2.0 * math.pi / FRAME)
    table = jnp.concatenate([jnp.cos(angle), -jnp.sin(angle)], axis=1) * FRAME ** (-0.5)
    weights = tap_weights.astype(jnp.float32)

    def block(total, segment):
        start = segment * S_DEV
        own = lax.dynamic_slice_in_dim(frames, start, S_DEV, 1)
        before = lax.dynamic_slice_in_dim(frames, jnp.maximum(start - (TAPS - 1), 0).astype(jnp.int32), TAPS - 1, 1)
        before = jnp.where(segment > 0, before, jnp.zeros_like(before))
        extended = jnp.concatenate([before, own], axis=1).astype(jnp.float32)
        filtered = weights[0][None, None, :] * extended[:, 0:S_DEV, :]
        for tap in range(1, TAPS):
            filtered = filtered + weights[tap][None, None, :] * extended[:, tap:tap + S_DEV, :]
        spectra = jnp.einsum('isn,nj->ijs', filtered, table, precision=lax.Precision.HIGHEST).astype(jnp.bfloat16)
        spec_f = spectra.astype(jnp.float32).reshape(INPUTS, 2, CHANNELS, S_DEV)
        real_part = jnp.einsum('ipcs,jpcs->icj', spec_f, spec_f)
        imag_part = jnp.einsum('ics,jcs->icj', spec_f[:, 1], spec_f[:, 0]) - jnp.einsum('ics,jcs->icj', spec_f[:, 0], spec_f[:, 1])
        return (total + jnp.stack([real_part, imag_part], axis=1), None)
    start_total = jnp.zeros((INPUTS, 2, CHANNELS, INPUTS), jnp.float32)
    total, _ = lax.scan(block, start_total, jnp.arange(N_TM, dtype=jnp.int32))
    return total * (1.0 / math.sqrt(NSPEC))
```

```python
import functools
import math

import jax
import jax.numpy as jnp
from jax import lax
from jax.experimental import pallas as pl
from jax.experimental.pallas import tpu as pltpu
from jax.sharding import PartitionSpec as P

MESH = pl.DeviceIdType.MESH
STEPS = 8
AHEAD = 2


def passed_along(block, axis, distance):
    devices = range(lax.axis_size(axis))
    route = [(i - distance, i) for i in devices if i - distance in devices]
    return lax.ppermute(block, axis, route)


def filter_taps(extended, weights, count):
    total = weights[0][None, None, :] * extended[:, 0:count, :].astype(jnp.float32)
    for tap in range(1, weights.shape[0]):
        total = total + weights[tap][None, None, :] * extended[:, tap : tap + count, :].astype(
            jnp.float32
        )
    return total


def exchange_and_correlate(
    n_inp, n_tm, steps, scale, spec, out, recv, part, got, send_sem, recv_sem, own_sem, put_sem, got_sem
):
    me = lax.axis_index("inp")
    seg = lax.axis_index("tm")
    ch_dev, _, in_dev, width = recv.shape
    per = ch_dev // steps
    inputs = n_inp * in_dev
    rows = inputs // n_tm
    half = width // 2

    barrier = pltpu.get_barrier_semaphore()
    for d in range(1, n_inp):
        pl.semaphore_signal(
            barrier, inc=1, device_id={"inp": lax.rem(me + d, n_inp)}, device_id_type=MESH
        )
    for d in range(1, n_tm):
        pl.semaphore_signal(
            barrier, inc=1, device_id={"tm": lax.rem(seg + d, n_tm)}, device_id_type=MESH
        )
    pl.semaphore_wait(barrier, n_inp - 1 + n_tm - 1)

    def own_copy(g):
        chunk = pl.ds(g * per, per)
        return pltpu.make_async_copy(spec.at[me, chunk], recv.at[chunk, me], own_sem.at[g])

    def turn_copy(g, d):
        chunk = pl.ds(g * per, per)
        peer = lax.rem(me + d, n_inp)
        return pltpu.make_async_remote_copy(
            src_ref=spec.at[peer, chunk],
            dst_ref=recv.at[chunk, me],
            send_sem=send_sem.at[g, d - 1],
            recv_sem=recv_sem.at[g, d - 1],
            device_id={"inp": peer},
            device_id_type=MESH,
        )

    def sum_copy(g, d):
        chunk = pl.ds(g * per, per)
        peer = lax.rem(seg + d, n_tm)
        return pltpu.make_async_remote_copy(
            src_ref=part.at[peer, chunk],
            dst_ref=got.at[d - 1, chunk],
            send_sem=put_sem.at[g, d - 1],
            recv_sem=got_sem.at[g, d - 1],
            device_id={"tm": peer},
            device_id_type=MESH,
        )

    def each(first, end, body):
        def step(d, carry):
            body(d)
            return carry

        lax.fori_loop(first, end, step, 0)

    def send(g):
        own_copy(g).start()
        each(1, n_inp, lambda d: turn_copy(g, d).start())

    def correlate(ch):
        block = recv[ch]
        if in_dev % 16 == 0:
            x = block.reshape(inputs, width)
        else:
            x = block.astype(jnp.float32).reshape(inputs, width).astype(jnp.bfloat16)
        y = jnp.concatenate([x[:, half:], -x[:, :half]], axis=1)
        for p, left in ((0, x), (1, y)):
            product = lax.dot_general(
                left, x, (((1,), (1,)), ((), ())), preferred_element_type=jnp.float32
            )
            for q in range(n_tm):
                part[q, ch, p] = product[q * rows : (q + 1) * rows]

    def finish(g):
        each(1, n_tm, lambda d: sum_copy(g, d).wait_recv())

        def add(k):
            ch = g * per + k
            total = part[seg, ch]
            for d in range(1, n_tm):
                total = total + got[d - 1, ch]
            out[ch] = total * scale

        each(0, per, add)

    for g in range(min(AHEAD, steps)):
        send(g)

    def step(g):
        @pl.when(g + AHEAD < steps)
        def _():
            send(g + AHEAD)

        own_copy(g).wait()
        each(1, n_inp, lambda d: turn_copy(g, d).wait_recv())
        each(0, per, lambda k: correlate(g * per + k))
        each(1, n_tm, lambda d: sum_copy(g, d).start())

        @pl.when(g >= 1)
        def _():
            finish(g - 1)

    each(0, steps, step)
    finish(steps - 1)

    def drain(g):
        each(1, n_inp, lambda d: turn_copy(g, d).wait_send())
        each(1, n_tm, lambda d: sum_copy(g, d).wait_send())

    each(0, steps, drain)


def per_device(samples, tap_weights):
    in_dev = samples.shape[0]
    frame = tap_weights.shape[1]
    taps = tap_weights.shape[0]
    rim = taps - 1
    spectra_dev = samples.shape[1] // frame
    frames = samples.reshape(in_dev, spectra_dev, frame)
    before = passed_along(frames[:, spectra_dev - rim :, :], "tm", 1)
    filtered = filter_taps(jnp.concatenate([before, frames], axis=1), tap_weights, spectra_dev)
    n_inp = lax.axis_size("inp")
    n_tm = lax.axis_size("tm")
    ch_dev = frame // 2 // n_inp
    column = jnp.arange(frame, dtype=jnp.int32)
    channel = column // 2
    is_real = column % 2 == 0
    index_n = jnp.arange(frame, dtype=jnp.int32)
    phase = index_n[:, None] * channel[None, :] % frame
    angle = phase.astype(jnp.float32) * (2.0 * math.pi / frame)
    table = jnp.where(is_real[None, :], jnp.cos(angle), -jnp.sin(angle)) * frame ** (-0.5)
    spectra = jnp.einsum(
        "isn,nj->ijs",
        filtered,
        table,
        precision=lax.Precision.HIGH,
        preferred_element_type=jnp.float32,
    ).astype(jnp.bfloat16)
    spectra = spectra.reshape(in_dev, n_inp, ch_dev, 2 * spectra_dev).transpose(1, 2, 0, 3)
    steps = math.gcd(STEPS, ch_dev)
    inputs = n_inp * in_dev
    rows = inputs // n_tm
    scale = 1.0 / math.sqrt(spectra_dev * n_tm)
    mine = pl.pallas_call(
        functools.partial(exchange_and_correlate, n_inp, n_tm, steps, scale),
        out_shape=jax.ShapeDtypeStruct((ch_dev, 2, rows, inputs), jnp.float32),
        in_specs=[pl.BlockSpec(memory_space=pltpu.HBM)],
        out_specs=pl.BlockSpec(memory_space=pltpu.VMEM),
        scratch_shapes=[
            pltpu.VMEM((ch_dev, n_inp, in_dev, 2 * spectra_dev), jnp.bfloat16),
            pltpu.VMEM((n_tm, ch_dev, 2, rows, inputs), jnp.float32),
            pltpu.VMEM((n_tm - 1, ch_dev, 2, rows, inputs), jnp.float32),
            pltpu.SemaphoreType.DMA((steps, n_inp - 1)),
            pltpu.SemaphoreType.DMA((steps, n_inp - 1)),
            pltpu.SemaphoreType.DMA((steps,)),
            pltpu.SemaphoreType.DMA((steps, n_tm - 1)),
            pltpu.SemaphoreType.DMA((steps, n_tm - 1)),
        ],
        compiler_params=pltpu.CompilerParams(
            collective_id=0, has_side_effects=True, vmem_limit_bytes=60 << 20
        ),
    )(spectra)
    return mine.transpose(2, 1, 0, 3)


def solution(mesh):
    return jax.shard_map(
        per_device,
        mesh=mesh,
        in_specs=(P("inp", "tm"), P()),
        out_specs=P("tm", None, "inp", None),
        check_vma=False,
    )
```

```python
import functools
import math

import jax
import jax.numpy as jnp
import numpy as np
from jax import lax
from jax.experimental import pallas as pl
from jax.experimental.pallas import tpu as pltpu
from jax.sharding import PartitionSpec as P

MESH = pl.DeviceIdType.MESH
STEPS = 16
AHEAD = 4


def passed_along(block, axis, distance):
    devices = range(lax.axis_size(axis))
    route = [(i - distance, i) for i in devices if i - distance in devices]
    return lax.ppermute(block, axis, route)


def filter_taps(extended, weights, count):
    total = weights[0][None, None, :] * extended[:, 0:count, :].astype(jnp.float32)
    for tap in range(1, weights.shape[0]):
        total = total + weights[tap][None, None, :] * extended[:, tap : tap + count, :].astype(
            jnp.float32
        )
    return total


def exchange_and_correlate(
    n_inp, n_tm, steps, scale, even, odd, out, recv, part, got, send_sem, recv_sem, own_sem, put_sem, got_sem
):
    me = lax.axis_index("inp")
    seg = lax.axis_index("tm")
    ch_dev, _, _, in_dev, count = recv.shape
    per = ch_dev // steps
    inputs = n_inp * in_dev
    rows = inputs // n_tm
    fold = ch_dev // 2
    turn = steps // 2

    barrier = pltpu.get_barrier_semaphore()
    for d in range(1, n_inp):
        pl.semaphore_signal(
            barrier, inc=1, device_id={"inp": lax.rem(me + d, n_inp)}, device_id_type=MESH
        )
    for d in range(1, n_tm):
        pl.semaphore_signal(
            barrier, inc=1, device_id={"tm": lax.rem(seg + d, n_tm)}, device_id_type=MESH
        )
    pl.semaphore_wait(barrier, n_inp - 1 + n_tm - 1)

    def own_copy(g, spec=even, at=0):
        return pltpu.make_async_copy(
            spec.at[me, pl.ds(at * per, per)], recv.at[pl.ds(g * per, per), :, me], own_sem.at[g]
        )

    def turn_copy(g, d, spec=even, at=0):
        peer = lax.rem(me + d, n_inp)
        return pltpu.make_async_remote_copy(
            src_ref=spec.at[peer, pl.ds(at * per, per)],
            dst_ref=recv.at[pl.ds(g * per, per), :, me],
            send_sem=send_sem.at[g, d - 1],
            recv_sem=recv_sem.at[g, d - 1],
            device_id={"inp": peer},
            device_id_type=MESH,
        )

    def sum_copy(g, d):
        chunk = pl.ds(g * per, per)
        peer = lax.rem(seg + d, n_tm)
        return pltpu.make_async_remote_copy(
            src_ref=part.at[peer, chunk],
            dst_ref=got.at[d - 1, chunk],
            send_sem=put_sem.at[g, d - 1],
            recv_sem=got_sem.at[g, d - 1],
            device_id={"tm": peer},
            device_id_type=MESH,
        )

    def each(first, end, body):
        def step(d, carry):
            body(d)
            return carry

        lax.fori_loop(first, end, step, 0)

    def send_from(g, spec, at):
        own_copy(g, spec, at).start()
        each(1, n_inp, lambda d: turn_copy(g, d, spec, at).start())

    def send(g):
        @pl.when(g < turn)
        def _():
            send_from(g, even, g)

        @pl.when(g >= turn)
        def _():
            send_from(g, odd, g - turn)

    def side(ch, p):
        block = recv[ch, p]
        if in_dev % 16 == 0:
            return block.reshape(inputs, count)
        return block.astype(jnp.float32).reshape(inputs, count).astype(jnp.bfloat16)

    def correlate(ch):
        real = side(ch, 0)
        imag = side(ch, 1)
        x = jnp.concatenate([real, imag], axis=1)
        y = jnp.concatenate([imag, -real], axis=1)
        for p, left in ((0, x), (1, y)):
            product = lax.dot_general(
                left, x, (((1,), (1,)), ((), ())), preferred_element_type=jnp.float32
            )
            for q in range(n_tm):
                part[q, ch, p] = product[q * rows : (q + 1) * rows]

    def finish(g):
        each(1, n_tm, lambda d: sum_copy(g, d).wait_recv())

        def add(k):
            ch = g * per + k
            total = part[seg, ch]
            for d in range(1, n_tm):
                total = total + got[d - 1, ch]
            out[lax.rem(ch, fold) * 2 + ch // fold] = total * scale

        each(0, per, add)

    for g in range(min(AHEAD, steps)):
        send(g)

    def step(g):
        @pl.when(g + AHEAD < steps)
        def _():
            send(g + AHEAD)

        own_copy(g).wait()
        each(1, n_inp, lambda d: turn_copy(g, d).wait_recv())
        each(0, per, lambda k: correlate(g * per + k))
        each(1, n_tm, lambda d: sum_copy(g, d).start())

        @pl.when(g >= 1)
        def _():
            finish(g - 1)

    each(0, steps, step)
    finish(steps - 1)

    def drain(g):
        each(1, n_inp, lambda d: turn_copy(g, d).wait_send())
        each(1, n_tm, lambda d: sum_copy(g, d).wait_send())

    each(0, steps, drain)


def per_device(samples, tap_weights):
    in_dev = samples.shape[0]
    frame = tap_weights.shape[1]
    taps = tap_weights.shape[0]
    rim = taps - 1
    spectra_dev = samples.shape[1] // frame
    frames = samples.reshape(in_dev, spectra_dev, frame)
    before = passed_along(frames[:, spectra_dev - rim :, :], "tm", 1)
    filtered = filter_taps(jnp.concatenate([before, frames], axis=1), tap_weights, spectra_dev)
    n_inp = lax.axis_size("inp")
    n_tm = lax.axis_size("tm")
    ch_dev = frame // 2 // n_inp
    fold = frame // 2
    low, high = filtered[:, :, :fold], filtered[:, :, fold:]
    sides = []
    for odd, folded in ((0, low + high), (1, low - high)):
        column = np.arange(fold)
        channel = column // 2 * 2 + odd
        phase = np.arange(fold)[:, None] * channel[None, :] % frame
        angle = phase * (2.0 * math.pi / frame)
        table = np.where(column % 2 == 0, np.cos(angle), -np.sin(angle)) * frame ** (-0.5)
        side = jnp.einsum(
            "isn,nj->ijs",
            folded,
            jnp.asarray(table, jnp.float32),
            precision=lax.Precision.HIGH,
            preferred_element_type=jnp.float32,
        ).astype(jnp.bfloat16)
        side = side.reshape(in_dev, n_inp, ch_dev // 2, 2, spectra_dev)
        sides.append(side.transpose(1, 2, 3, 0, 4))
    steps = math.gcd(STEPS, ch_dev)
    inputs = n_inp * in_dev
    rows = inputs // n_tm
    scale = 1.0 / math.sqrt(spectra_dev * n_tm)
    mine = pl.pallas_call(
        functools.partial(exchange_and_correlate, n_inp, n_tm, steps, scale),
        out_shape=jax.ShapeDtypeStruct((ch_dev, 2, rows, inputs), jnp.float32),
        in_specs=[pl.BlockSpec(memory_space=pltpu.HBM)] * 2,
        out_specs=pl.BlockSpec(memory_space=pltpu.VMEM),
        scratch_shapes=[
            pltpu.VMEM((ch_dev, 2, n_inp, in_dev, spectra_dev), jnp.bfloat16),
            pltpu.VMEM((n_tm, ch_dev, 2, rows, inputs), jnp.float32),
            pltpu.VMEM((n_tm - 1, ch_dev, 2, rows, inputs), jnp.float32),
            pltpu.SemaphoreType.DMA((steps, n_inp - 1)),
            pltpu.SemaphoreType.DMA((steps, n_inp - 1)),
            pltpu.SemaphoreType.DMA((steps,)),
            pltpu.SemaphoreType.DMA((steps, n_tm - 1)),
            pltpu.SemaphoreType.DMA((steps, n_tm - 1)),
        ],
        compiler_params=pltpu.CompilerParams(
            collective_id=0, has_side_effects=True, vmem_limit_bytes=60 << 20
        ),
    )(*sides)
    return mine.transpose(2, 1, 0, 3)


def solution(mesh):
    return jax.shard_map(
        per_device,
        mesh=mesh,
        in_specs=(P("inp", "tm"), P()),
        out_specs=P("tm", None, "inp", None),
        check_vma=False,
    )
```

```python
import functools
import math

import jax
import jax.numpy as jnp
import numpy as np
from jax import lax
from jax.experimental import pallas as pl
from jax.experimental.pallas import tpu as pltpu
from jax.sharding import PartitionSpec as P

MESH = pl.DeviceIdType.MESH
STEPS = 16
AHEAD = 4


def passed_along(block, axis, distance):
    devices = range(lax.axis_size(axis))
    route = [(i - distance, i) for i in devices if i - distance in devices]
    return lax.ppermute(block, axis, route)


def filter_taps(extended, weights, count):
    total = weights[0][None, None, :] * extended[:, 0:count, :].astype(jnp.float32)
    for tap in range(1, weights.shape[0]):
        total = total + weights[tap][None, None, :] * extended[:, tap : tap + count, :].astype(
            jnp.float32
        )
    return total


def exchange_and_correlate(
    n_inp, n_tm, steps, scale, even, odd, out, recv, part, got, send_sem, recv_sem, own_sem, put_sem, got_sem
):
    me = lax.axis_index("inp")
    seg = lax.axis_index("tm")
    ch_dev, _, _, in_dev, count = recv.shape
    per = ch_dev // steps
    inputs = n_inp * in_dev
    rows = inputs // n_tm
    fold = ch_dev // 2
    turn = steps // 2

    barrier = pltpu.get_barrier_semaphore()
    for d in range(1, n_inp):
        pl.semaphore_signal(
            barrier, inc=1, device_id={"inp": lax.rem(me + d, n_inp)}, device_id_type=MESH
        )
    for d in range(1, n_tm):
        pl.semaphore_signal(
            barrier, inc=1, device_id={"tm": lax.rem(seg + d, n_tm)}, device_id_type=MESH
        )
    pl.semaphore_wait(barrier, n_inp - 1 + n_tm - 1)

    def own_copy(g, spec=even, at=0):
        return pltpu.make_async_copy(
            spec.at[me, pl.ds(at * per, per)], recv.at[pl.ds(g * per, per), :, me], own_sem.at[g]
        )

    def turn_copy(g, d, spec=even, at=0):
        peer = lax.rem(me + d, n_inp)
        return pltpu.make_async_remote_copy(
            src_ref=spec.at[peer, pl.ds(at * per, per)],
            dst_ref=recv.at[pl.ds(g * per, per), :, me],
            send_sem=send_sem.at[g, d - 1],
            recv_sem=recv_sem.at[g, d - 1],
            device_id={"inp": peer},
            device_id_type=MESH,
        )

    def sum_copy(g, d):
        chunk = pl.ds(g * per, per)
        peer = lax.rem(seg + d, n_tm)
        return pltpu.make_async_remote_copy(
            src_ref=part.at[peer, chunk],
            dst_ref=got.at[d - 1, chunk],
            send_sem=put_sem.at[g, d - 1],
            recv_sem=got_sem.at[g, d - 1],
            device_id={"tm": peer},
            device_id_type=MESH,
        )

    def each(first, end, body):
        def step(d, carry):
            body(d)
            return carry

        lax.fori_loop(first, end, step, 0)

    def send_from(g, spec, at):
        own_copy(g, spec, at).start()
        first = n_inp // 2 - 1
        each(
            0,
            n_inp - 1,
            lambda k: turn_copy(g, 1 + lax.rem(k + first, n_inp - 1), spec, at).start(),
        )

    def send(g):
        @pl.when(g < turn)
        def _():
            send_from(g, even, g)

        @pl.when(g >= turn)
        def _():
            send_from(g, odd, g - turn)

    def side(ch, p):
        block = recv[ch, p]
        if in_dev % 16 == 0:
            return block.reshape(inputs, count)
        return block.astype(jnp.float32).reshape(inputs, count).astype(jnp.bfloat16)

    def correlate(ch):
        real = side(ch, 0)
        imag = side(ch, 1)
        x = jnp.concatenate([real, imag], axis=1)
        y = jnp.concatenate([imag, -real], axis=1)
        for p, left in ((0, x), (1, y)):
            product = lax.dot_general(
                left, x, (((1,), (1,)), ((), ())), preferred_element_type=jnp.float32
            )
            for q in range(n_tm):
                part[q, ch, p] = product[q * rows : (q + 1) * rows]

    def finish(g):
        each(1, n_tm, lambda d: sum_copy(g, d).wait_recv())

        def add(k):
            ch = g * per + k
            total = part[seg, ch]
            for d in range(1, n_tm):
                total = total + got[d - 1, ch]
            out[lax.rem(ch, fold) * 2 + ch // fold] = total * scale

        each(0, per, add)

    for g in range(min(AHEAD, steps)):
        send(g)

    def step(g):
        @pl.when(g + AHEAD < steps)
        def _():
            send(g + AHEAD)

        own_copy(g).wait()
        each(1, n_inp, lambda d: turn_copy(g, d).wait_recv())
        each(0, per, lambda k: correlate(g * per + k))
        each(1, n_tm, lambda d: sum_copy(g, d).start())

        @pl.when(g >= 1)
        def _():
            finish(g - 1)

    each(0, steps, step)
    finish(steps - 1)

    def drain(g):
        each(1, n_inp, lambda d: turn_copy(g, d).wait_send())
        each(1, n_tm, lambda d: sum_copy(g, d).wait_send())

    each(0, steps, drain)


def per_device(samples, tap_weights):
    in_dev = samples.shape[0]
    frame = tap_weights.shape[1]
    taps = tap_weights.shape[0]
    rim = taps - 1
    spectra_dev = samples.shape[1] // frame
    frames = samples.reshape(in_dev, spectra_dev, frame)
    before = passed_along(frames[:, spectra_dev - rim :, :], "tm", 1)
    filtered = filter_taps(jnp.concatenate([before, frames], axis=1), tap_weights, spectra_dev)
    n_inp = lax.axis_size("inp")
    n_tm = lax.axis_size("tm")
    ch_dev = frame // 2 // n_inp
    fold = frame // 2
    low, high = filtered[:, :, :fold], filtered[:, :, fold:]
    sides = []
    for odd, folded in ((0, low + high), (1, low - high)):
        column = np.arange(fold)
        channel = column // 2 * 2 + odd
        phase = np.arange(fold)[:, None] * channel[None, :] % frame
        angle = phase * (2.0 * math.pi / frame)
        table = np.where(column % 2 == 0, np.cos(angle), -np.sin(angle)) * frame ** (-0.5)
        side = jnp.einsum(
            "isn,nj->ijs",
            folded,
            jnp.asarray(table, jnp.float32),
            precision=lax.Precision.HIGH,
            preferred_element_type=jnp.float32,
        ).astype(jnp.bfloat16)
        side = side.reshape(in_dev, n_inp, ch_dev // 2, 2, spectra_dev)
        sides.append(side.transpose(1, 2, 3, 0, 4))
    steps = math.gcd(STEPS, ch_dev)
    inputs = n_inp * in_dev
    rows = inputs // n_tm
    scale = 1.0 / math.sqrt(spectra_dev * n_tm)
    mine = pl.pallas_call(
        functools.partial(exchange_and_correlate, n_inp, n_tm, steps, scale),
        out_shape=jax.ShapeDtypeStruct((ch_dev, 2, rows, inputs), jnp.float32),
        in_specs=[pl.BlockSpec(memory_space=pltpu.HBM)] * 2,
        out_specs=pl.BlockSpec(memory_space=pltpu.VMEM),
        scratch_shapes=[
            pltpu.VMEM((ch_dev, 2, n_inp, in_dev, spectra_dev), jnp.bfloat16),
            pltpu.VMEM((n_tm, ch_dev, 2, rows, inputs), jnp.float32),
            pltpu.VMEM((n_tm - 1, ch_dev, 2, rows, inputs), jnp.float32),
            pltpu.SemaphoreType.DMA((steps, n_inp - 1)),
            pltpu.SemaphoreType.DMA((steps, n_inp - 1)),
            pltpu.SemaphoreType.DMA((steps,)),
            pltpu.SemaphoreType.DMA((steps, n_tm - 1)),
            pltpu.SemaphoreType.DMA((steps, n_tm - 1)),
        ],
        compiler_params=pltpu.CompilerParams(
            collective_id=0, has_side_effects=True, vmem_limit_bytes=60 << 20
        ),
    )(*sides)
    return mine.transpose(2, 1, 0, 3)


def solution(mesh):
    return jax.shard_map(
        per_device,
        mesh=mesh,
        in_specs=(P("inp", "tm"), P()),
        out_specs=P("tm", None, "inp", None),
        check_vma=False,
    )
```
